32 devices in a mesh: groups: 2 (over x), expert: 16 (over z, y, core).
Axes of the slice: x: 2, y: 2, z: 4, core: 2. Of those that a mesh axis runs over, the one named last changes fastest.
Arguments:
- tokens: bfloat16 [512, 2048], P(('groups', 'expert')), parts along dimension 0, may hold values from -6 to 6
- depths: int32 [512], P(('groups', 'expert')), parts along dimension 0, may hold values from 1 to 2
- routes: int32 [2, 512, 8], P(None, ('groups', 'expert')), parts along dimension 1, may hold values from 0 to 15, all different within a row; in each aligned block of 16 rows (0 to 15, 16 to 31, ..., all dimensions but the last counted through in order) at most 16 rows name the same one
- norm_gain: bfloat16 [2048], replicated, may hold values from 0.099609375 to 1.8984375
- router: bfloat16 [2048, 16], replicated, may hold values from -0.125 to 0.125
- w_gate: bfloat16 [16, 2048, 768], P('expert'), may hold values from -0.125 to 0.125
- w_up: bfloat16 [16, 2048, 768], P('expert'), may hold values from -0.125 to 0.125
- w_down: bfloat16 [16, 768, 2048], P('expert'), may hold values from -0.21875 to 0.21875
- replica_plan: int32 [16], replicated, may hold values from 0 to 15, as said below
- copy_choice: int32 [16, 16], P('expert'), may hold values from 0 to 15, as said below
Outputs:
- final_state: bfloat16 [512, 2048], P(('groups', 'expert')), parts along dimension 0
- copy_load: float32 [32, 4], P(('groups', 'expert')), parts along dimension 0
The draws below stay inside these ranges and needn't reach their ends.
There are 2 independent parts, one for each index of `groups`. The reference program is written for one: setup_inputs(seed, part) draws one part's arguments, and reference() takes and returns one part's arrays. A program takes and returns all parts, laid end to end along the dimension named above; an argument that names none is the same for every part. Nothing has to cross between parts.
Inputs may be any that keep to these rules, and one draw needn't show every extreme that they name: `routes`: in each pass the 8 experts of a row differ, and no expert is named by more than 16 rows of one device (an aligned block of 16 rows); some expert is named by exactly 16 rows in some blocks. replica_plan[d] is never d. copy_choice[s, e] is a device number.
All inputs are finite; a program needn't handle non-finite values.
Results may differ from the reference program's by a relative error of at most 0.0038.
The reference program's roundings to bfloat16 on the way count: a program that leaves them out, or rounds other values in their place, can miss the bound.
Values may be sent and summed in bfloat16 or wider, within the bound.
No kernel may reach another device: no remote copies, remote signals or barrier semaphores. Data moves between devices by JAX's collectives and lax.ppermute only.
A program may use at most 64 MiB of HBM per device.

```python
import math
import jax
import jax.numpy as jnp
import numpy as np
from jax import lax

D = 2048
FF = 768
TOP = 8
ITERS = 2
TOK_DEV = 16
EXPERTS = 16
MOST = 16
TOKENS = 256
N_EXPERT = 16


def make_plan(key):
    hot_count = EXPERTS // 8
    order = jax.random.permutation(jax.random.fold_in(key, 11), EXPERTS).astype(jnp.int32)
    hot_list = order[:hot_count]
    choose = jax.random.randint(jax.random.fold_in(key, 12), (EXPERTS,), 0, hot_count)
    device_ids = jnp.arange(EXPERTS, dtype=jnp.int32)
    first = hot_list[choose]
    second = hot_list[(choose + 1) % hot_count]
    return jnp.where(first == device_ids, second, first).astype(jnp.int32)


def draw_replica_plan(key, part):
    return make_plan(key)


def draw_copy_choice(key, part):
    plan_table = make_plan(key)
    ident = jnp.arange(EXPERTS, dtype=jnp.int32)
    holds = (plan_table[None, :] == ident[:, None]).astype(jnp.int32)
    ranks = jnp.cumsum(holds, axis=1) * holds
    copies = 1 + jnp.sum(holds, axis=1)
    pick_copy = jax.random.randint(jax.random.fold_in(key, 13), (EXPERTS, EXPERTS), 0, copies[None, :])
    match = (ranks[None, :, :] == pick_copy[:, :, None]) & (holds[None, :, :] == 1)
    other = jnp.sum(jnp.where(match, ident[None, None, :], 0), axis=2)
    return jnp.where(pick_copy == 0, ident[None, :], other).astype(jnp.int32)


def plant(result, rng, low, largest):
    place = [jax.random.randint(jax.random.fold_in(rng, axis), (), 0, length) for axis, length in enumerate(result.shape)]
    main_axis = result.shape.index(max(result.shape))
    beside = place[:main_axis] + [(place[main_axis] + 1) % result.shape[main_axis]] + place[main_axis + 1:]
    return result.at[tuple(place)].set(low).at[tuple(beside)].set(largest)


def shard_levels(rng, extent, cuts, least, top_value):
    def one(dim, shards_of):
        heights = jax.random.uniform(jax.random.fold_in(jax.random.fold_in(rng, 6), dim), (shards_of,), jnp.float32, least / len(cuts), top_value / len(cuts))
        return jnp.repeat(jnp.exp(heights), extent[dim] // shards_of).reshape((-1,) + (1,) * (len(extent) - dim - 1))

    factor_of = one(*cuts[0])
    for cut in cuts[1:]:
        factor_of = factor_of * one(*cut)
    return factor_of


def shared_out(key, own, number, rows, number_of, top, most, slope):
    sequence = jax.random.permutation(key, number_of)
    packed, ordinary = portions_of(number_of, rows * top, most, slope, True), portions_of(number_of, rows * top, most, slope, False)
    places = jnp.arange(number_of)

    def named(lengths, offset_by):
        used = int((lengths > 0).sum())
        fixed = max(1, used // 4)
        shifted = fixed + (places - fixed + offset_by * (used - fixed)) % max(1, number_of - fixed)
        return jnp.zeros((number_of,), jnp.int32).at[sequence[jnp.where(places < fixed, places, shifted)]].set(jnp.asarray(lengths, jnp.int32))

    lengths = jnp.where(number % 4 == 0, named(packed, number // 4), named(ordinary, number - number // 4 - 1))
    mixed = jax.random.permutation(jax.random.fold_in(own, 3), number_of)
    giver, receiver = mixed[0:number_of // 2 * 2:2], mixed[1:number_of // 2 * 2:2]
    slack = jnp.minimum(lengths[giver] - 1, most - lengths[receiver]) // 2
    slack = jnp.where((giver == sequence[0]) | (receiver == sequence[0]) | (lengths[receiver] == 0), 0, jnp.maximum(slack, 0))
    shifted = jax.random.randint(jax.random.fold_in(own, 4), (number_of // 2,), 0, 1 << 20) % (slack + 1)
    lengths = lengths.at[giver].add(-shifted).at[receiver].add(shifted)
    labels = jnp.searchsorted(jnp.cumsum(lengths), jnp.arange(rows * top), side="right").astype(jnp.int32)
    listing = labels.reshape(top, rows).T
    listing = listing[jax.random.permutation(jax.random.fold_in(own, 1), rows)]
    offset_by = jax.random.randint(jax.random.fold_in(own, 2), (rows, 1), 0, top)
    return jnp.take_along_axis(listing, (jnp.arange(top)[None, :] + offset_by) % top, axis=1)


def portions_of(amount, total, limit, slope, full):
    portions = [(1 << 20) // math.isqrt(grade ** slope) + 1 for grade in range(1, amount + 1)]
    largest = limit if full else min(limit, max(-(-total // amount), total * portions[0] // sum(portions)))
    least = 1 if total - largest >= amount - 1 else 0
    given, spare = [largest] + [least] * (amount - 1), total - largest - least * (amount - 1)
    while spare > 0:
        movable = [i for i in range(1, amount) if given[i] < largest] or [i for i in range(1, amount) if given[i] < limit]
        mass, budget = sum([portions[i] for i in movable]), spare
        for i in movable:
            more = min(limit - given[i], max(1, budget * portions[i] // mass), spare)
            given[i] = given[i] + more
            spare = spare - more
    return np.array(given)


def scatter_about(key, dims, scale, limit, split=(), held_as=jnp.bfloat16):
    array = jax.random.normal(key, dims, jnp.float32) * scale
    if len(split) > 0:
        array = shard_levels(key, dims, split, -0.22, 0.18) * array
    return jnp.clip(array, min=-limit, max=limit).astype(held_as)


def setup_inputs(seed: int = 0, part: int = 0) -> dict:
    key_of = jax.random.split(jax.random.key(seed), 11)
    part_splits = jax.random.split(jax.random.fold_in(key_of[10], part), 11)
    tokens = scatter_about(part_splits[0], (TOKENS, D), 1.0, 6.0, ((0, 16),))
    depths = plant(jax.random.randint(part_splits[1], (TOKENS,), 1, 3), jax.random.fold_in(part_splits[1], 1), 1, 2).astype(jnp.int32)
    routes_keys = jax.random.split(jax.random.fold_in(part_splits[2], 1), ITERS * TOKENS // TOK_DEV)
    routes_turns = jax.random.permutation(jax.random.fold_in(part_splits[2], 3), ITERS * TOKENS // TOK_DEV)
    routes = jax.vmap(lambda own, number: shared_out(jax.random.fold_in(part_splits[2], 2), own, number, TOK_DEV, EXPERTS, TOP, MOST, 2))(routes_keys, routes_turns).reshape((ITERS, TOKENS, TOP))
    norm_gain = jnp.clip(1.0 + 0.18 * jax.random.normal(key_of[3], (D,), jnp.float32), 0.099609375, 1.8984375).astype(jnp.bfloat16)
    router = scatter_about(key_of[4], (D, EXPERTS), D ** -0.5, 0.125)
    w_gate = scatter_about(key_of[5], (EXPERTS, D, FF), D ** -0.5, 0.125, ((0, 16),))
    w_up = scatter_about(key_of[6], (EXPERTS, D, FF), D ** -0.5, 0.125, ((0, 16),))
    w_down = scatter_about(key_of[7], (EXPERTS, FF, D), FF ** -0.5, 0.21875, ((0, 16),))
    replica_plan = draw_replica_plan(jax.random.fold_in(key_of[10], 71), part)
    copy_choice = draw_copy_choice(jax.random.fold_in(key_of[10], 71), part)
    return dict(tokens=tokens, depths=depths, routes=routes, norm_gain=norm_gain, router=router, w_gate=w_gate, w_up=w_up, w_down=w_down, replica_plan=replica_plan, copy_choice=copy_choice)


def expert_block(pieces):
    rows_in, gate_w, up_w, down_w = pieces
    highest = lax.Precision.HIGHEST
    gate_val = jnp.dot(rows_in.astype(jnp.float32), gate_w.astype(jnp.float32), precision=highest)
    up_val = jnp.dot(rows_in.astype(jnp.float32), up_w.astype(jnp.float32), precision=highest)
    hidden = (jax.nn.silu(gate_val) * up_val).astype(jnp.bfloat16)
    return jnp.dot(hidden.astype(jnp.float32), down_w.astype(jnp.float32), precision=highest).astype(jnp.bfloat16)

def reference(tokens, depths, routes, norm_gain, router, w_gate, w_up, w_down, replica_plan, copy_choice):
    highest = lax.Precision.HIGHEST
    capacity = N_EXPERT * MOST
    state = tokens
    row_ids = jnp.arange(TOKENS, dtype=jnp.int32)
    source = row_ids // TOK_DEV
    expert_ids = jnp.arange(EXPERTS, dtype=jnp.int32)
    pair_rows = jnp.broadcast_to(row_ids[:, None], (TOKENS, TOP)).reshape(-1)
    loads = []
    for layer_step in range(ITERS):
        state32 = state.astype(jnp.float32)
        scale = lax.rsqrt(lax.optimization_barrier(jnp.mean(state32 * state32, axis=1, keepdims=True)) + 1e-06)
        normed = (state32 * scale * norm_gain.astype(jnp.float32)).astype(jnp.bfloat16)
        logits = jnp.dot(normed, router, preferred_element_type=jnp.float32)
        chosen = routes[layer_step]
        picked = jnp.take_along_axis(logits, chosen, axis=1)
        sigmas = jax.nn.sigmoid(picked)
        gates = sigmas / lax.optimization_barrier(jnp.sum(sigmas, axis=1, keepdims=True))
        active = depths > layer_step
        onehot = (chosen[:, :, None] == expert_ids).astype(jnp.int32)
        ranks = jnp.cumsum(onehot.reshape(N_EXPERT, TOK_DEV * TOP, EXPERTS), axis=1).reshape(TOKENS, TOP, EXPERTS)
        position = lax.optimization_barrier(jnp.sum(ranks * onehot, axis=2)) - 1
        slot_index = (chosen * capacity + source[:, None] * MOST + position).reshape(-1).astype(jnp.int32)
        table = jnp.full((EXPERTS * capacity,), TOKENS, jnp.int32).at[slot_index].set(pair_rows)
        padded = jnp.concatenate([normed, jnp.zeros((1, D), jnp.bfloat16)], axis=0)

        def one_expert(pieces):
            index_rows, gate_w, up_w, down_w = pieces
            return expert_block((padded[index_rows], gate_w, up_w, down_w))
        outputs = lax.map(one_expert, (table.reshape(EXPERTS, capacity), w_gate, w_up, w_down))
        pair_out = outputs.reshape(EXPERTS * capacity, D)[slot_index].reshape(TOKENS, TOP, D)
        weights = gates * active[:, None].astype(jnp.float32)
        delta = jnp.einsum('rk,rkd->rd', weights, pair_out.astype(jnp.float32), precision=highest)
        state = (state32 + delta).astype(jnp.bfloat16)
        wanted = copy_choice[source[:, None], chosen]
        valid = (replica_plan[wanted] == chosen) & (wanted != chosen)
        target = jnp.where(valid, wanted, chosen).astype(jnp.int32)
        slot_bit = valid.astype(jnp.int32)
        bucket = (target * 2 + slot_bit).reshape(-1)
        live = jnp.broadcast_to(active[:, None], (TOKENS, TOP)).reshape(-1).astype(jnp.float32)
        counts = jax.ops.segment_sum(live, bucket, num_segments=2 * EXPERTS)
        loads.append(counts.reshape(EXPERTS, 2))
    copy_load = jnp.concatenate(loads, axis=1) / float(TOK_DEV * TOP)
    return (state, copy_load)
```

```python
import functools

import jax
import jax.numpy as jnp
from jax import lax
from jax.experimental import pallas as pl
from jax.experimental.pallas import tpu as pltpu
from jax.sharding import PartitionSpec as P

LANES = 128
BF16 = jnp.bfloat16
F32 = jnp.float32


def expert_ffn(rows_in, gate_w, up_w, down_w):
    gate_val = jnp.dot(rows_in, gate_w, preferred_element_type=jnp.float32)
    up_val = jnp.dot(rows_in, up_w, preferred_element_type=jnp.float32)
    hidden = (jax.nn.silu(gate_val) * up_val).astype(jnp.bfloat16)
    return jnp.dot(hidden, down_w, preferred_element_type=jnp.float32).astype(jnp.bfloat16)


def sparse_body(
    tokens, depths, routes, norm_gain, router, w_gate, w_up, w_down, replica_plan, copy_choice
):
    highest = lax.Precision.HIGHEST
    peer_count = lax.axis_size("expert")
    row_count, model_width = tokens.shape
    iter_count, _, top_count = routes.shape
    cap_rows = 2 * row_count * top_count // peer_count
    expert_ids = jnp.arange(peer_count, dtype=jnp.int32)
    copy_row = copy_choice[0]
    home_gate, home_up, home_down = (w_gate[0], w_up[0], w_down[0])
    onehot_all = routes[:, :, :, None] == expert_ids
    wanted_all = jnp.sum(jnp.where(onehot_all, copy_row, 0), axis=3)
    plan_at = jnp.sum(jnp.where(wanted_all[..., None] == expert_ids, replica_plan, 0), axis=3)
    valid_all = (plan_at == routes) & (wanted_all != routes)
    target_all = jnp.where(valid_all, wanted_all, routes)
    slot_all = valid_all.astype(jnp.int32)
    active_all = depths[None, :] > jnp.arange(iter_count, dtype=jnp.int32)[:, None]
    live_all = jnp.broadcast_to(active_all[:, :, None], routes.shape)
    bucket_all = target_all * 2 + slot_all
    bucket_hot = (bucket_all[..., None] == jnp.arange(2 * peer_count, dtype=jnp.int32)) & live_all[
        ..., None
    ]
    counts = jnp.sum(bucket_hot.astype(jnp.float32), axis=(1, 2)).reshape(iter_count, peer_count, 2)
    counts = jnp.transpose(counts, (1, 0, 2)).reshape(peer_count, 2 * iter_count)
    copy_load = lax.psum_scatter(counts, "expert", scatter_dimension=0, tiled=True) / float(
        row_count * top_count
    )
    pair_rows = jnp.repeat(jnp.arange(row_count, dtype=jnp.int32), top_count)
    buffer_rows = peer_count * cap_rows
    state = tokens
    for layer_step in range(iter_count):
        state32 = state.astype(jnp.float32)
        scale = lax.rsqrt(jnp.mean(state32 * state32, axis=1, keepdims=True) + 1e-06)
        normed = (state32 * scale * norm_gain.astype(jnp.float32)).astype(jnp.bfloat16)
        logits = jnp.dot(normed, router, preferred_element_type=jnp.float32)
        picked = jnp.sum(jnp.where(onehot_all[layer_step], logits[:, None, :], 0.0), axis=2)
        sigmas = jax.nn.sigmoid(picked)
        gates = sigmas / jnp.sum(sigmas, axis=1, keepdims=True)
        target_dev = routes[layer_step]
        live_pairs = live_all[layer_step].reshape(-1)
        bucket = target_dev.reshape(-1)
        bucket_flags = (
            (bucket[:, None] == jnp.arange(peer_count, dtype=jnp.int32)) & live_pairs[:, None]
        ).astype(jnp.int32)
        rank_table = jnp.cumsum(bucket_flags, axis=0)
        position = jnp.sum(rank_table * bucket_flags, axis=1) - 1
        index_flat = target_dev.reshape(-1) * cap_rows + position
        send_index = jnp.where(live_pairs, index_flat, buffer_rows)
        outbound = (
            jnp.zeros((buffer_rows, model_width), jnp.bfloat16)
            .at[send_index]
            .set(normed[pair_rows], mode="drop")
        )
        outbound = outbound.reshape(peer_count, cap_rows, 1, model_width)
        received = lax.all_to_all(outbound, "expert", split_axis=0, concat_axis=0, tiled=True)
        first_rows = received.reshape(buffer_rows, model_width)
        result = expert_ffn(first_rows, home_gate, home_up, home_down).reshape(outbound.shape)
        returned = lax.all_to_all(result, "expert", split_axis=0, concat_axis=0, tiled=True)
        read_index = jnp.where(live_pairs, index_flat, 0)
        pair_out = returned.reshape(buffer_rows, model_width)[read_index].reshape(
            row_count, top_count, model_width
        )
        weights = gates * live_all[layer_step].astype(jnp.float32)
        delta = jnp.einsum("rk,rkd->rd", weights, pair_out.astype(jnp.float32), precision=highest)
        state = (state32 + delta).astype(jnp.bfloat16)
    return (state, copy_load)


def ffn_kernel(step, x_ref, meta_ref, router_ref, gate_ref, up_ref, down_ref, own_ref, other_ref,
               hidden_ref):
    rows, width = x_ref.shape
    top = 8
    ff = gate_ref.shape[-1]
    experts = router_ref.shape[1]
    me = lax.axis_index("expert")
    x = x_ref[...]
    logits = jnp.dot(x, router_ref[...], preferred_element_type=F32)
    sig = jax.nn.sigmoid(logits)
    meta = meta_ref[...].astype(F32)
    ids = lax.broadcasted_iota(jnp.int32, (rows, experts), 1)
    idf = ids.astype(F32)
    named = jnp.zeros((rows, experts), F32)
    for k in range(top):
        c = step * top + k
        named = jnp.where(meta[:, c:c + 1] == idf, 1.0, named)
    sig = jnp.where(named > 0.0, sig, 0.0)
    total = jnp.sum(sig, axis=1, keepdims=True)
    mine = jnp.sum(jnp.where(ids == me, sig, 0.0), axis=1, keepdims=True)
    depth = meta[:, 2 * top:2 * top + 1]
    weight = jnp.where(depth > float(step), mine / total, 0.0)

    tile = 256

    @pl.loop(0, ff // tile)
    def _(i):
        cols = pl.ds(pl.multiple_of(i * tile, tile), tile)
        g = jnp.dot(x_ref[...], gate_ref[0, :, cols], preferred_element_type=F32)
        u = jnp.dot(x_ref[...], up_ref[0, :, cols], preferred_element_type=F32)
        hidden_ref[:, cols] = (g * jax.nn.sigmoid(g) * u).astype(BF16)

    half = rows // 2

    @pl.loop(0, width // tile)
    def _(i):
        cols = pl.ds(pl.multiple_of(i * tile, tile), tile)
        o = jnp.dot(hidden_ref[...], down_ref[0, :, cols], preferred_element_type=F32)
        o = o.astype(BF16).astype(F32) * weight
        own_ref[:, cols] = o[:half].astype(BF16)
        other_ref[:, cols] = o[half:].astype(BF16)


def run_ffn(step, x, meta, router, w_gate, w_up, w_down):
    rows, width = x.shape
    ff = w_gate.shape[-1]
    half = jax.ShapeDtypeStruct((rows // 2, width), BF16)
    return pl.pallas_call(
        functools.partial(ffn_kernel, step),
        out_shape=(half, half),
        in_specs=[pl.BlockSpec(memory_space=pltpu.VMEM)] * 6,
        out_specs=(pl.BlockSpec(memory_space=pltpu.VMEM),) * 2,
        scratch_shapes=[pltpu.VMEM((rows, ff), BF16)],
        cost_estimate=pl.CostEstimate(
            flops=6 * rows * width * ff, bytes_accessed=6 * width * ff, transcendentals=rows * ff
        ),
        name=f"ffn{step}",
    )(x, meta, router, w_gate, w_up, w_down)


def dense_body(
    tokens, depths, routes, norm_gain, router, w_gate, w_up, w_down, replica_plan, copy_choice
):
    n = lax.axis_size("expert")
    rows, width = tokens.shape
    iters, _, top = routes.shape
    chips = n // 2
    ny = 1
    while (2 * ny) * (2 * ny) <= chips:
        ny *= 2
    nz = chips // ny
    zs = 2 * ny

    def swap(x, offset):
        return lax.ppermute(x, "expert", [(i, i ^ offset) for i in range(n)])

    def gather(x):
        zb = [x] + [swap(x, a * zs) for a in range(1, nz)]
        z_all = jnp.concatenate(zb, 0)
        plane = jnp.concatenate([z_all] + [swap(z_all, b * 2) for b in range(1, ny)], 0)
        return jnp.concatenate([plane, swap(plane, 1)], 0)

    def scatter(own, other):
        plane = own.astype(F32) + swap(other, 1).astype(F32)
        r = rows * nz
        acc = plane[:r]
        for b in range(1, ny):
            acc = acc + swap(plane[b * r:(b + 1) * r].astype(BF16), b * 2).astype(F32)
        out = acc[:rows]
        for a in range(1, nz):
            out = out + swap(acc[a * rows:(a + 1) * rows].astype(BF16), a * zs).astype(F32)
        return out

    pieces = [routes[t] for t in range(iters)] + [
        depths[:, None],
        jnp.broadcast_to(copy_choice, (rows, n)),
    ]
    used = iters * top + 1 + n
    meta = jnp.concatenate(pieces + [jnp.zeros((rows, LANES - used), jnp.int32)], 1).astype(BF16)

    me = lax.axis_index("expert")
    state = tokens
    meta_all = None
    for step in range(iters):
        state32 = state.astype(F32)
        scale = lax.rsqrt(jnp.mean(state32 * state32, axis=1, keepdims=True) + 1e-06)
        normed = (state32 * scale * norm_gain.astype(F32)).astype(BF16)
        if step == 0:
            both = gather(jnp.concatenate([normed, meta], 1))
            x_all, meta_all = both[:, :width], both[:, width:]
        else:
            x_all = gather(normed)
        own, other = run_ffn(step, x_all, meta_all, router, w_gate, w_up, w_down)
        state = (state32 + scatter(own, other)).astype(BF16)

    info = meta_all.astype(jnp.int32)
    depth_all = info[:, iters * top]
    copies = info[:, iters * top + 1:iters * top + 1 + n]
    ids = jnp.arange(n, dtype=jnp.int32)
    second = replica_plan[me]
    home_copy = jnp.sum(jnp.where(ids == me, copies, 0), axis=1)
    home_plan = jnp.sum(jnp.where(home_copy[:, None] == ids, replica_plan, 0), axis=1)
    home_away = (home_plan == me) & (home_copy != me)
    here = jnp.sum(jnp.where(ids == second, copies, 0), axis=1) == me
    loads = []
    for t in range(iters):
        live = depth_all > t
        picks = info[:, t * top:(t + 1) * top]
        names_me = jnp.any(picks == me, axis=1)
        names_second = jnp.any(picks == second, axis=1) & (second != me)
        loads.append(jnp.sum((live & names_me & ~home_away).astype(F32)))
        loads.append(jnp.sum((live & names_second & here).astype(F32)))
    copy_load = jnp.stack(loads)[None, :] / float(rows * top)
    return (state, copy_load)


def body(tokens, depths, routes, *rest):
    n = lax.axis_size("expert")
    rows = tokens.shape[0]
    iters, _, top = routes.shape
    dense = 2 * rows * top // n >= rows and iters * top + 1 + n <= LANES and n % 4 == 0
    return (dense_body if dense else sparse_body)(tokens, depths, routes, *rest)


def solution(mesh):
    return jax.shard_map(
        body,
        mesh=mesh,
        in_specs=(
            P(("groups", "expert"), None),
            P(("groups", "expert")),
            P(None, ("groups", "expert"), None),
            P(),
            P(),
            P("expert", None, None),
            P("expert", None, None),
            P("expert", None, None),
            P(),
            P("expert", None),
        ),
        out_specs=(P(("groups", "expert"), None), P(("groups", "expert"), None)),
        check_vma=False,
    )
```

```python
import functools

import jax
import jax.numpy as jnp
from jax import lax
from jax.experimental import pallas as pl
from jax.experimental.pallas import tpu as pltpu
from jax.sharding import PartitionSpec as P

LANES = 128
BF16 = jnp.bfloat16
F32 = jnp.float32


def expert_ffn(rows_in, gate_w, up_w, down_w):
    gate_val = jnp.dot(rows_in, gate_w, preferred_element_type=jnp.float32)
    up_val = jnp.dot(rows_in, up_w, preferred_element_type=jnp.float32)
    hidden = (jax.nn.silu(gate_val) * up_val).astype(jnp.bfloat16)
    return jnp.dot(hidden, down_w, preferred_element_type=jnp.float32).astype(jnp.bfloat16)


def sparse_body(
    tokens, depths, routes, norm_gain, router, w_gate, w_up, w_down, replica_plan, copy_choice
):
    highest = lax.Precision.HIGHEST
    peer_count = lax.axis_size("expert")
    row_count, model_width = tokens.shape
    iter_count, _, top_count = routes.shape
    cap_rows = 2 * row_count * top_count // peer_count
    expert_ids = jnp.arange(peer_count, dtype=jnp.int32)
    copy_row = copy_choice[0]
    home_gate, home_up, home_down = (w_gate[0], w_up[0], w_down[0])
    onehot_all = routes[:, :, :, None] == expert_ids
    wanted_all = jnp.sum(jnp.where(onehot_all, copy_row, 0), axis=3)
    plan_at = jnp.sum(jnp.where(wanted_all[..., None] == expert_ids, replica_plan, 0), axis=3)
    valid_all = (plan_at == routes) & (wanted_all != routes)
    target_all = jnp.where(valid_all, wanted_all, routes)
    slot_all = valid_all.astype(jnp.int32)
    active_all = depths[None, :] > jnp.arange(iter_count, dtype=jnp.int32)[:, None]
    live_all = jnp.broadcast_to(active_all[:, :, None], routes.shape)
    bucket_all = target_all * 2 + slot_all
    bucket_hot = (bucket_all[..., None] == jnp.arange(2 * peer_count, dtype=jnp.int32)) & live_all[
        ..., None
    ]
    counts = jnp.sum(bucket_hot.astype(jnp.float32), axis=(1, 2)).reshape(iter_count, peer_count, 2)
    counts = jnp.transpose(counts, (1, 0, 2)).reshape(peer_count, 2 * iter_count)
    copy_load = lax.psum_scatter(counts, "expert", scatter_dimension=0, tiled=True) / float(
        row_count * top_count
    )
    pair_rows = jnp.repeat(jnp.arange(row_count, dtype=jnp.int32), top_count)
    buffer_rows = peer_count * cap_rows
    state = tokens
    for layer_step in range(iter_count):
        state32 = state.astype(jnp.float32)
        scale = lax.rsqrt(jnp.mean(state32 * state32, axis=1, keepdims=True) + 1e-06)
        normed = (state32 * scale * norm_gain.astype(jnp.float32)).astype(jnp.bfloat16)
        logits = jnp.dot(normed, router, preferred_element_type=jnp.float32)
        picked = jnp.sum(jnp.where(onehot_all[layer_step], logits[:, None, :], 0.0), axis=2)
        sigmas = jax.nn.sigmoid(picked)
        gates = sigmas / jnp.sum(sigmas, axis=1, keepdims=True)
        target_dev = routes[layer_step]
        live_pairs = live_all[layer_step].reshape(-1)
        bucket = target_dev.reshape(-1)
        bucket_flags = (
            (bucket[:, None] == jnp.arange(peer_count, dtype=jnp.int32)) & live_pairs[:, None]
        ).astype(jnp.int32)
        rank_table = jnp.cumsum(bucket_flags, axis=0)
        position = jnp.sum(rank_table * bucket_flags, axis=1) - 1
        index_flat = target_dev.reshape(-1) * cap_rows + position
        send_index = jnp.where(live_pairs, index_flat, buffer_rows)
        outbound = (
            jnp.zeros((buffer_rows, model_width), jnp.bfloat16)
            .at[send_index]
            .set(normed[pair_rows], mode="drop")
        )
        outbound = outbound.reshape(peer_count, cap_rows, 1, model_width)
        received = lax.all_to_all(outbound, "expert", split_axis=0, concat_axis=0, tiled=True)
        first_rows = received.reshape(buffer_rows, model_width)
        result = expert_ffn(first_rows, home_gate, home_up, home_down).reshape(outbound.shape)
        returned = lax.all_to_all(result, "expert", split_axis=0, concat_axis=0, tiled=True)
        read_index = jnp.where(live_pairs, index_flat, 0)
        pair_out = returned.reshape(buffer_rows, model_width)[read_index].reshape(
            row_count, top_count, model_width
        )
        weights = gates * live_all[layer_step].astype(jnp.float32)
        delta = jnp.einsum("rk,rkd->rd", weights, pair_out.astype(jnp.float32), precision=highest)
        state = (state32 + delta).astype(jnp.bfloat16)
    return (state, copy_load)


VMEM = pl.BlockSpec(memory_space=pltpu.VMEM)
HBM = pl.BlockSpec(memory_space=pltpu.HBM)


def dot_t(a, b):
    return lax.dot_general(a, b, (((1,), (1,)), ((), ())), preferred_element_type=F32)


def norm_rows(state32, gain):
    mean = jnp.mean(state32 * state32, axis=1, keepdims=True)
    return (state32 * lax.rsqrt(mean + 1e-06) * gain).astype(BF16)


def open_kernel(*refs):
    args, out_ref, held, sems = refs[:5], refs[5], refs[6:11], refs[11]
    moves = [pltpu.make_async_copy(a, h, sems.at[i]) for i, (a, h) in enumerate(zip(args, held))]
    for m in moves:
        m.start()
    for m in moves:
        m.wait()
    tokens_ref, gain_ref, routes_ref, depths_ref, copies_ref = held
    rows, width = tokens_ref.shape
    iters, top, _ = routes_ref.shape
    n = copies_ref.shape[1]
    out_ref[:, :width] = norm_rows(
        tokens_ref[...].astype(F32), gain_ref[...].astype(F32).reshape(1, width)
    )
    expert = lax.broadcasted_iota(jnp.int32, (n, rows), 0)
    parts = []
    for t in range(iters):
        live = depths_ref[...] > t
        named = jnp.zeros((n, rows), F32)
        for k in range(top):
            named = jnp.where((routes_ref[t, k:k + 1, :] == expert) & live, 1.0, named)
        parts.append(named)
    square = (n, n)
    diag = lax.broadcasted_iota(jnp.int32, square, 0) == lax.broadcasted_iota(jnp.int32, square, 1)
    copies = jnp.where(diag, jnp.broadcast_to(copies_ref[...], square).astype(F32), 0.0)
    parts.append(jnp.broadcast_to(jnp.sum(copies, axis=1, keepdims=True), (n, rows)))
    parts.append(jnp.zeros((LANES - (iters + 1) * n, rows), F32))
    table = jnp.concatenate(parts, 0).astype(BF16)
    square = (rows, rows)
    eye = lax.broadcasted_iota(jnp.int32, square, 0) == lax.broadcasted_iota(jnp.int32, square, 1)
    meta = dot_t(jnp.where(eye, 1.0, 0.0).astype(BF16), table)
    out_ref[:, width:] = meta.astype(BF16)


def run_open(tokens, gain, routes, depths, copies):
    rows, width = tokens.shape
    args = tuple(pltpu.with_memory_space_constraint(x, pltpu.HBM) for x in (tokens, gain, routes, depths, copies))
    return pl.pallas_call(
        open_kernel,
        out_shape=jax.ShapeDtypeStruct((rows, width + LANES), BF16),
        in_specs=[HBM] * 5,
        out_specs=VMEM,
        scratch_shapes=[pltpu.VMEM(x.shape, x.dtype) for x in args]
        + [pltpu.SemaphoreType.DMA((len(args),))],
        compiler_params=pltpu.CompilerParams(vmem_limit_bytes=4 << 20),
        name="open_rows",
    )(*args)


CHUNKS = 4


def load_kernel(*refs):
    count = len(refs) // 2
    sems = refs[-1]
    copies = []
    for i in range(count):
        src, dst = refs[i], refs[count + i]
        size = src.shape[1] // CHUNKS
        for j in range(CHUNKS):
            part = pl.ds(j * size, size)
            copies.append(
                pltpu.make_async_copy(src.at[:, part], dst.at[:, part], sems.at[i, j])
            )
    for c in copies:
        c.start()
    for c in copies:
        c.wait()


def run_load(*weights):
    size = sum(w.size for w in weights)
    weights = tuple(pltpu.with_memory_space_constraint(w, pltpu.HBM) for w in weights)
    return pl.pallas_call(
        load_kernel,
        out_shape=tuple(jax.ShapeDtypeStruct(w.shape, w.dtype) for w in weights),
        in_specs=[HBM] * len(weights),
        out_specs=(VMEM,) * len(weights),
        scratch_shapes=[pltpu.SemaphoreType.DMA((len(weights), CHUNKS))],
        compiler_params=pltpu.CompilerParams(vmem_limit_bytes=1 << 20),
        cost_estimate=pl.CostEstimate(flops=0, bytes_accessed=4 * size, transcendentals=0),
        name="load_weights",
    )(*weights)


def count_kernel(iters, scale, meta_ref, plan_ref, load_ref):
    meta_col = meta_ref.shape[1] - LANES
    n = plan_ref.shape[1]
    me = lax.axis_index("expert").astype(F32)
    meta = meta_ref[:, meta_col:].astype(F32)
    rows = meta.shape[0]
    lane = lax.broadcasted_iota(jnp.int32, (rows, LANES), 1).astype(F32)
    ids = lax.broadcasted_iota(jnp.int32, (rows, n), 1).astype(F32)
    plan = jnp.broadcast_to(plan_ref[...].astype(F32), (rows, n))

    def at(index):
        return jnp.sum(jnp.where(lane == index, meta, 0.0), axis=1, keepdims=True)

    first = float(iters * n)
    second = jnp.sum(jnp.where(ids == me, plan, 0.0), axis=1, keepdims=True)
    home_copy = at(me + first)
    home_plan = jnp.sum(jnp.where(ids == home_copy, plan, 0.0), axis=1, keepdims=True)
    at_home = jnp.where((home_plan == me) & (home_copy != me), 0.0, 1.0)
    at_copy = jnp.where((at(second + first) == me) & (second != me), 1.0, 0.0)
    slot = lax.broadcasted_iota(jnp.int32, (1, 2 * iters), 1)
    loads = jnp.zeros((1, 2 * iters), F32)
    for t in range(iters):
        for j, (which, served) in enumerate(((me, at_home), (second, at_copy))):
            pairs = jnp.sum(at(which + float(t * n)) * served, axis=0, keepdims=True)
            loads = jnp.where(slot == 2 * t + j, pairs, loads)
    load_ref[...] = loads / scale


def run_count(iters, scale, meta, plan):
    return pl.pallas_call(
        functools.partial(count_kernel, iters, scale),
        out_shape=jax.ShapeDtypeStruct((1, 2 * iters), F32),
        in_specs=[VMEM] * 2,
        out_specs=VMEM,
        compiler_params=pltpu.CompilerParams(vmem_limit_bytes=4 << 20),
        cost_estimate=pl.CostEstimate(flops=0, bytes_accessed=1 << 20, transcendentals=0),
        name="count_pairs",
    )(meta, plan)


def ffn_kernel(step, x_ref, meta_ref, router_ref, gate_ref, up_ref, down_ref,
               own_ref, other_ref, hidden_ref):
    rows = x_ref.shape[0]
    width, ff = gate_ref.shape[1:]
    n = router_ref.shape[0]
    meta_col = meta_ref.shape[1] - LANES
    me = lax.axis_index("expert")

    routers = jnp.concatenate([router_ref[...]] * (LANES // n), 0)
    logits = dot_t(x_ref[:, :width], routers)
    lane = lax.broadcasted_iota(jnp.int32, (rows, LANES), 1)
    named = (meta_ref[:, meta_col:].astype(F32) > 0.0) & (lane >= step * n) & (lane < (step + 1) * n)
    sig = jnp.where(named, jax.nn.sigmoid(logits), 0.0)
    total = jnp.sum(sig, axis=1, keepdims=True)
    at_me = lane == step * n + me
    mine = jnp.sum(jnp.where(at_me, sig, 0.0), axis=1, keepdims=True)
    here = jnp.sum(jnp.where(at_me & named, 1.0, 0.0), axis=1, keepdims=True)
    weight = jnp.where(here > 0.0, mine / total, 0.0)

    g = jnp.dot(x_ref[:, :width], gate_ref[0], preferred_element_type=F32)
    u = jnp.dot(x_ref[:, :width], up_ref[0], preferred_element_type=F32)
    hidden_ref[...] = (g * jax.nn.sigmoid(g) * u).astype(BF16)

    half = rows // 2
    tile = 512

    @pl.loop(0, width // tile)
    def _(i):
        cols = pl.ds(pl.multiple_of(i * tile, tile), tile)
        o = jnp.dot(hidden_ref[...], down_ref[0, :, cols], preferred_element_type=F32)
        o = o.astype(BF16).astype(F32) * weight
        own_ref[:, cols] = o[:half]
        other_ref[:, cols] = o[half:].astype(BF16)


def run_ffn(step, x, meta, router, w_gate, w_up, w_down):
    rows = x.shape[0]
    width, ff = w_gate.shape[1:]
    return pl.pallas_call(
        functools.partial(ffn_kernel, step),
        out_shape=(
            jax.ShapeDtypeStruct((rows // 2, width), F32),
            jax.ShapeDtypeStruct((rows // 2, width), BF16),
        ),
        in_specs=[VMEM] * 6,
        out_specs=(VMEM,) * 2,
        scratch_shapes=[pltpu.VMEM((rows, ff), BF16)],
        compiler_params=pltpu.CompilerParams(vmem_limit_bytes=16 << 20),
        cost_estimate=pl.CostEstimate(
            flops=6 * rows * width * ff, bytes_accessed=4 * rows * width, transcendentals=rows * ff
        ),
        name=f"ffn{step}",
    )(x, meta, router, w_gate, w_up, w_down)


def dense_body(
    tokens, depths, routes, norm_gain, router, w_gate, w_up, w_down, replica_plan, copy_choice
):
    n = lax.axis_size("expert")
    rows, width = tokens.shape
    iters, _, top = routes.shape
    chips = n // 2
    ny = 1
    while (2 * ny) * (2 * ny) <= chips:
        ny *= 2
    nz = chips // ny
    zs = 2 * ny
    gain = norm_gain[None, :]

    def swap(x, offset):
        return lax.ppermute(x, "expert", [(i, i ^ offset) for i in range(n)])

    def gather(x, beside=()):
        zb = [x] + [swap(x, a * zs) for a in range(1, nz)]
        zb, beside = lax.optimization_barrier((zb, beside))
        z_all = jnp.concatenate(zb, 0)
        plane = jnp.concatenate([z_all] + [swap(z_all, b * 2) for b in range(1, ny)], 0)
        return jnp.concatenate([plane, swap(plane, 1)], 0), beside

    def scatter(own, other):
        plane = own + swap(other, 1).astype(F32)
        r = rows * nz
        acc = plane[:r]
        for b in range(1, ny):
            acc = acc + swap(plane[b * r:(b + 1) * r].astype(BF16), b * 2).astype(F32)
        out = acc[:rows]
        for a in range(1, nz):
            out = out + swap(acc[a * rows:(a + 1) * rows].astype(BF16), a * zs).astype(F32)
        return out

    block = run_open(
        tokens, norm_gain, jnp.transpose(routes, (0, 2, 1)), depths[None, :], copy_choice
    )
    block, w_gate, w_up, w_down = lax.optimization_barrier((block, w_gate, w_up, w_down))
    weights = run_load(w_gate, w_up, w_down)
    state = tokens
    meta = None
    for step in range(iters):
        x_all, weights = gather(block, weights)
        if step == 0:
            meta = x_all
            copy_load = run_count(iters, float(rows * top), meta, replica_plan[None, :])
        own, other = run_ffn(step, x_all, meta, router.T, *weights)
        state = (state.astype(F32) + scatter(own, other)).astype(BF16)
        block = norm_rows(state.astype(F32), gain.astype(F32))
    return (state, copy_load)


def body(tokens, depths, routes, *rest):
    n = lax.axis_size("expert")
    rows = tokens.shape[0]
    iters, _, top = routes.shape
    dense = 2 * rows * top // n >= rows and (iters + 1) * n <= LANES and LANES % n == 0 and n % 4 == 0
    return (dense_body if dense else sparse_body)(tokens, depths, routes, *rest)


def solution(mesh):
    return jax.shard_map(
        body,
        mesh=mesh,
        in_specs=(
            P(("groups", "expert"), None),
            P(("groups", "expert")),
            P(None, ("groups", "expert"), None),
            P(),
            P(),
            P("expert", None, None),
            P("expert", None, None),
            P("expert", None, None),
            P(),
            P("expert", None),
        ),
        out_specs=(P(("groups", "expert"), None), P(("groups", "expert"), None)),
        check_vma=False,
    )
```
